32 devices in a mesh: segment: 4 (over y, x), chan: 8 (over z, core).
Axes of the slice: x: 2, y: 2, z: 4, core: 2. Of those that a mesh axis runs over, the one named last changes fastest.
Arguments:
- resident: float32 [4, 1280, 512], P('segment', 'chan'), may hold values from -6 to 6
- held_skip: float32 [4, 1280, 512], P('segment', 'chan'), may hold values from -6 to 6
- fresh: float32 [2, 1280, 512], P(None, 'chan'), may hold values from -6 to 6
- first_weight: float32 [4, 1280, 11520], P('segment', 'chan'), may hold values from -0.0546875 to 0.0546875
- second_weight: float32 [4, 1280, 11520], P('segment', 'chan'), may hold values from -0.0546875 to 0.0546875
Outputs:
- last_outputs: float32 [4, 1280, 512], P('segment', 'chan')
The draws below stay inside these ranges and needn't reach their ends.
All inputs are finite; a program needn't handle non-finite values.
Results may differ from the reference program's by a relative error of at most 0.0001.
Values sent between devices are 32-bit elements; how exact they have to be, the bound alone decides.
A program may use at most 128 MiB of HBM per device.

```python
import jax
import jax.numpy as jnp
from jax import lax

C = 1280
ROWS = 16
COLS = 32
TICKS = 3
P_SIZE = 512
SECTIONS = 4


def block_levels(key, dims, shards, least, high):
    def one(position, parts):
        draws = jax.random.uniform(jax.random.fold_in(jax.random.fold_in(key, 6), position), (parts,), jnp.float32, least / len(shards), high / len(shards))
        return jnp.repeat(jnp.exp(draws), dims[position] // parts).reshape((-1,) + (1,) * (len(dims) - position - 1))

    factor_of = one(*shards[0])
    for cut in shards[1:]:
        factor_of = factor_of * one(*cut)
    return factor_of


def scatter_about(rng, dims, scale, most, pieces=(), dtype=jnp.bfloat16):
    entries = scale * jax.random.normal(rng, dims, jnp.float32)
    if pieces:
        entries = entries * block_levels(rng, dims, pieces, -0.22, 0.18)
    return jnp.clip(entries, -most, most).astype(dtype)


def setup_inputs(seed: int = 0) -> dict:
    streams_of = jax.random.split(jax.random.key(seed), 6)
    return {
        "resident": scatter_about(streams_of[0], (SECTIONS, C, P_SIZE), 1.0, 6.0, ((0, 4), (1, 8)), jnp.float32),
        "held_skip": scatter_about(streams_of[1], (SECTIONS, C, P_SIZE), 1.0, 6.0, ((0, 4), (1, 8)), jnp.float32),
        "fresh": scatter_about(streams_of[2], (TICKS - 1, C, P_SIZE), 1.0, 6.0, ((1, 8),), jnp.float32),
        "first_weight": scatter_about(streams_of[3], (SECTIONS, C, 9 * C), (9 * C) ** -0.5, 0.0546875, ((0, 4), (1, 8)), jnp.float32),
        "second_weight": scatter_about(streams_of[4], (SECTIONS, C, 9 * C), (9 * C) ** -0.5, 0.0546875, ((0, 4), (1, 8)), jnp.float32),
    }


def tap_shift(x, dy, dx):
    grid = x.reshape(x.shape[:-1] + (ROWS, COLS))
    padded = jnp.pad(grid, [(0, 0)] * (grid.ndim - 2) + [(1, 1), (1, 1)])
    moved = padded[..., 1 + dy:1 + dy + ROWS, 1 + dx:1 + dx + COLS]
    return moved.reshape(x.shape)


def convolve(weight, field):
    shifted = jnp.stack([tap_shift(field, dy, dx) for dy in (-1, 0, 1) for dx in (-1, 0, 1)])
    return jnp.dot(weight, shifted.reshape(9 * C, ROWS * COLS), precision=lax.Precision.HIGHEST, preferred_element_type=jnp.float32)


def section(inputs):
    w_first, w_second, field, skip, encoder = inputs
    first = convolve(w_first, field)
    operand = jnp.where(encoder, jax.nn.silu(first), skip)
    second = convolve(w_second, operand)
    return jnp.where(encoder, field + second, jax.nn.silu(first + second))


def reference(resident, held_skip, fresh, first_weight, second_weight):
    encoder = jnp.arange(SECTIONS) < SECTIONS // 2
    state = resident
    skip = held_skip
    outputs = resident
    for tick in range(TICKS):
        outputs = lax.map(section, (first_weight, second_weight, state, skip, encoder))
        if tick < TICKS - 1:
            state = jnp.concatenate([fresh[tick][None], outputs[:-1]], axis=0)
            skip = jnp.where(encoder[:, None, None], skip, outputs[::-1])
    return outputs
```

```python
import functools

import jax
import jax.numpy as jnp
from jax import lax
from jax.experimental import pallas as pl
from jax.experimental.pallas import tpu as pltpu
from jax.sharding import PartitionSpec as P

ROWS = 16
COLS = 32
MESH = pl.DeviceIdType.MESH


def silu(v):
    return v / (1.0 + jnp.exp(-v))


def block_of(rows):
    for size in (32, 40, 16):
        if rows % size == 0:
            return size
    return 8


def kernel(
    segments, n, ticks,
    resident, held_skip, fresh, weights, out_ref,
    wv, g, operand, acc, conv_first, passed_out,
    w_sem, recv_sem, send_sem, pass_send, pass_recv,
):
    seg = lax.axis_index("segment")
    me = lax.axis_index("chan")
    place = me // 2
    core = me % 2
    partner = me + 1 - 2 * core
    length = n // 2
    half = segments // 2
    encoder = seg < half
    rows, positions = resident.shape
    width = 2 * rows
    blk = block_of(rows)

    def load(conv, q):
        return pltpu.make_async_copy(weights.at[conv, q], wv.at[conv, q], w_sem.at[conv, q])

    def start_loads(conv):
        def one(q, _):
            load(conv, q).start()
            return 0
        lax.fori_loop(0, length, one, 0)

    start_loads(0)
    start_loads(1)

    barrier = pltpu.get_barrier_semaphore()

    def greet(cond, segment, chan):
        @pl.when(cond)
        def _():
            pl.semaphore_signal(barrier, inc=1, device_id=(segment, chan), device_id_type=MESH)
        return jnp.where(cond, 1, 0)

    greeted = greet(place > 0, seg, jnp.maximum(me - 2, 0))
    greeted += greet(place < length - 1, seg, jnp.minimum(me + 2, n - 1))
    greeted += greet(place >= 0, seg, partner)
    greeted += greet(seg > 0, jnp.maximum(seg - 1, 0), me)
    greeted += greet(seg < segments - 1, jnp.minimum(seg + 1, segments - 1), me)
    greeted += greet(seg >= 0, segments - 1 - seg, me)
    pl.semaphore_wait(barrier, greeted)

    def hop(k, j, way):
        target = (jnp.maximum(me - 2, 0), jnp.minimum(me + 2, n - 1), partner)[way]
        return pltpu.make_async_remote_copy(
            src_ref=g.at[k, j],
            dst_ref=g.at[k, j],
            send_sem=send_sem.at[way, j],
            recv_sem=recv_sem.at[k, j],
            device_id=(seg, target),
            device_id_type=MESH,
        )

    def give(t, kind):
        target = (jnp.minimum(seg + 1, segments - 1), segments - 1 - seg)[kind]
        return pltpu.make_async_remote_copy(
            src_ref=passed_out.at[t],
            dst_ref=g.at[2 * (t + 1) + kind, me],
            send_sem=pass_send.at[t, kind],
            recv_sem=pass_recv.at[t, kind],
            device_id=(target, me),
            device_id_type=MESH,
        )

    def multiply(k, conv, q, first):
        for i in range(2):
            part = g[k, 2 * q + i]
            high = part.astype(jnp.bfloat16)
            low = (part - high.astype(jnp.float32)).astype(jnp.bfloat16)
            operand[i * rows : (i + 1) * rows] = high
            operand[width + i * rows : width + (i + 1) * rows] = high
            operand[2 * width + i * rows : 2 * width + (i + 1) * rows] = low

        def group(m, _):
            product = jnp.dot(
                wv[conv, q, m], operand[...], preferred_element_type=jnp.float32
            )
            if first:
                acc[m] = product
            else:
                acc[m] += product
            return 0
        lax.fori_loop(0, 3, group, 0)

    def gather_and_multiply(k, conv):
        @pl.when(place < length - 1)
        def _():
            hop(k, me, 1).start()

        @pl.when(place > 0)
        def _():
            hop(k, me, 0).start()

        hop(k, me, 2).start()
        hop(k, partner, 2).wait_recv()
        if k < 2:
            load(conv, place).wait()
        multiply(k, conv, place, True)

        def step(d, _):
            for side in range(2):
                q = place - d if side == 0 else place + d
                there = q >= 0 if side == 0 else q < length
                onward = place < length - 1 if side == 0 else place > 0
                mine = 2 * q + core

                @pl.when(there)
                def _():
                    hop(k, mine, 2).wait_recv()

                    @pl.when(onward)
                    def _():
                        hop(k, mine, 1 - side).start()
                    hop(k, mine, 2).start()

            def one(side, _):
                q = place - d + 2 * d * side

                @pl.when((q >= 0) & (q < length))
                def _():
                    hop(k, 2 * q + 1 - core, 2).wait_recv()
                    if k < 2:
                        load(conv, q).wait()
                    multiply(k, conv, q, False)
                return 0
            lax.fori_loop(0, 2, one, 0)
            return 0
        lax.fori_loop(1, length, step, 0)

        def drain(q, _):
            j = 2 * q + core
            hop(k, j, 2).wait_send()

            @pl.when((q <= place) & (place < length - 1))
            def _():
                hop(k, j, 1).wait_send()

            @pl.when((q >= place) & (place > 0))
            def _():
                hop(k, j, 0).wait_send()
            return 0
        lax.fori_loop(0, length, drain, 0)

    spot = lax.broadcasted_iota(jnp.int32, (blk, positions), 1)
    column = spot % COLS

    def placed(start):
        total = None
        for dx in (-1, 0, 1):
            column_sum = None
            for dy in (-1, 0, 1):
                part = acc[dy + 1, pl.ds(pl.multiple_of((dx + 1) * rows + start, 8), blk), :]
                if dy:
                    part = pltpu.roll(part, (-dy * COLS) % positions, 1)
                    source = spot + dy * COLS
                    part = jnp.where((source >= 0) & (source < positions), part, 0.0)
                column_sum = part if column_sum is None else column_sum + part
            if dx:
                column_sum = pltpu.roll(column_sum, (-dx) % positions, 1)
                source = column + dx
                column_sum = jnp.where((source >= 0) & (source < COLS), column_sum, 0.0)
            total = column_sum if total is None else total + column_sum
        return total

    def over_rows(action):
        def one(i, _):
            start = pl.multiple_of(i * blk, 8)
            action(start, pl.ds(start, blk))
            return 0
        lax.fori_loop(0, rows // blk, one, 0)

    g[0, me] = resident[...]

    @pl.when(jnp.logical_not(encoder))
    def _():
        g[1, me] = held_skip[...]

    for t in range(ticks):
        k = 2 * t
        if t:
            @pl.when(seg > 0)
            def _():
                give(t - 1, 0).wait_recv()

            @pl.when(seg == 0)
            def _():
                g[k, me] = fresh[t - 1]

        gather_and_multiply(k, 0)

        def after_first(start, rows_of):
            value = placed(start)
            conv_first[rows_of, :] = value

            @pl.when(encoder)
            def _():
                g[k + 1, me, rows_of, :] = silu(value)
        over_rows(after_first)
        if t:
            @pl.when(jnp.logical_not(encoder))
            def _():
                give(t - 1, 1).wait_recv()

        gather_and_multiply(k + 1, 1)

        def after_second(start, rows_of):
            value = placed(start)

            @pl.when(encoder)
            def _():
                passed_out[t, rows_of, :] = g[k, me, rows_of, :] + value

            @pl.when(jnp.logical_not(encoder))
            def _():
                passed_out[t, rows_of, :] = silu(conv_first[rows_of, :] + value)
        over_rows(after_second)

        if t < ticks - 1:
            @pl.when(seg < segments - 1)
            def _():
                give(t, 0).start()

            @pl.when(encoder)
            def _():
                give(t, 1).start()

    for t in range(ticks - 1):
        @pl.when(seg < segments - 1)
        def _():
            give(t, 0).wait_send()

        @pl.when(encoder)
        def _():
            give(t, 1).wait_send()
    out_ref[...] = passed_out[ticks - 1]


def split_weight(weight, length):
    rows = weight.shape[0]
    width = weight.shape[1] // 9 // length
    high = lax.reduce_precision(weight, 8, 7)
    low = weight - high
    high, low = high.astype(jnp.bfloat16), low.astype(jnp.bfloat16)

    def by_piece(part):
        part = part.reshape(rows, 3, 3, length, width)
        return part.transpose(3, 1, 2, 0, 4).reshape(length, 3, 3 * rows, width)

    high, low = by_piece(high), by_piece(low)
    return jnp.concatenate([high, low, high], axis=-1)


def body(segments, n, resident, held_skip, fresh, first_weight, second_weight):
    ticks = fresh.shape[0] + 1
    rows, positions = resident.shape[1:]
    length = n // 2
    width = 2 * rows
    weights = jnp.stack([split_weight(first_weight[0], length), split_weight(second_weight[0], length)])
    vmem = pl.BlockSpec(memory_space=pltpu.VMEM)
    out = pl.pallas_call(
        functools.partial(kernel, segments, n, ticks),
        out_shape=jax.ShapeDtypeStruct((rows, positions), jnp.float32),
        in_specs=[vmem, vmem, vmem, pl.BlockSpec(memory_space=pl.ANY)],
        out_specs=vmem,
        scratch_shapes=[
            pltpu.VMEM((2, length, 3, 3 * rows, 3 * width), jnp.bfloat16),
            pltpu.VMEM((2 * ticks, n, rows, positions), jnp.float32),
            pltpu.VMEM((3 * width, positions), jnp.bfloat16),
            pltpu.VMEM((3, 3 * rows, positions), jnp.float32),
            pltpu.VMEM((rows, positions), jnp.float32),
            pltpu.VMEM((ticks, rows, positions), jnp.float32),
            pltpu.SemaphoreType.DMA((2, length)),
            pltpu.SemaphoreType.DMA((2 * ticks, n)),
            pltpu.SemaphoreType.DMA((3, n)),
            pltpu.SemaphoreType.DMA((ticks - 1, 2)),
            pltpu.SemaphoreType.DMA((ticks - 1, 2)),
        ],
        compiler_params=pltpu.CompilerParams(
            collective_id=0, has_side_effects=True, vmem_limit_bytes=60 * 1024 * 1024
        ),
    )(resident[0], held_skip[0], fresh, weights)
    return out[None]


def solution(mesh):
    return jax.shard_map(
        functools.partial(body, mesh.shape["segment"], mesh.shape["chan"]),
        mesh=mesh,
        in_specs=(
            P("segment", "chan", None),
            P("segment", "chan", None),
            P(None, "chan", None),
            P("segment", "chan", None),
            P("segment", "chan", None),
        ),
        out_specs=P("segment", "chan", None),
        check_vma=False,
    )
```

```python
import functools

import jax
import jax.numpy as jnp
from jax import lax
from jax.experimental import pallas as pl
from jax.experimental.pallas import tpu as pltpu
from jax.sharding import PartitionSpec as P

ROWS = 16
COLS = 32
MESH = pl.DeviceIdType.MESH


def silu(v):
    return v / (1.0 + jnp.exp(-v))


def block_of(rows):
    for size in (32, 40, 16):
        if rows % size == 0:
            return size
    return 8


HALVES = 2


def kernel(
    segments, n, ticks,
    resident, held_skip, fresh, first_weight, second_weight, out_ref,
    stage, wv, g, operand, acc, conv_first, passed_out,
    w_sem, recv_sem, send_sem, pass_send, pass_recv,
):
    seg = lax.axis_index("segment")
    me = lax.axis_index("chan")
    place = me // 2
    core = me % 2
    partner = me + 1 - 2 * core
    length = n // 2
    half = segments // 2
    encoder = seg < half
    shares_input = seg == half
    rows, positions = resident.shape
    part_positions = positions // HALVES
    width = 2 * rows
    channels = length * width
    blk = block_of(rows)
    split_blk = 32 if rows % 32 == 0 else rows

    def load(conv, tap):
        source = (first_weight, second_weight)[conv]
        columns = pl.ds(pl.multiple_of(tap * channels, 128), channels)
        return pltpu.make_async_copy(source.at[0, :, columns], stage.at[tap], w_sem.at[tap])

    def start_loads(conv):
        def one(tap, _):
            load(conv, tap).start()
            return 0
        lax.fori_loop(0, 9, one, 0)

    def split_weights(conv):
        def three_taps(y, _):
            for x in range(3):
                tap = 3 * y + x
                load(conv, tap).wait()

                def some_rows(i, _):
                    start = i * split_blk
                    if split_blk != rows:
                        start = pl.multiple_of(start, 16)
                    for q in range(length):
                        value = stage[tap, pl.ds(start, split_blk), q * width : (q + 1) * width]
                        high = value.astype(jnp.bfloat16)
                        low = (value - high.astype(jnp.float32)).astype(jnp.bfloat16)
                        spot = pl.ds(x * rows + start, split_blk)
                        if split_blk != rows:
                            spot = pl.ds(pl.multiple_of(x * rows + start, 16), split_blk)
                        wv[conv, q, y, spot, 0:width] = high
                        wv[conv, q, y, spot, width : 2 * width] = low
                        wv[conv, q, y, spot, 2 * width : 3 * width] = high
                    return 0
                if split_blk == rows:
                    some_rows(0, 0)
                else:
                    lax.fori_loop(0, rows // split_blk, some_rows, 0)
            return 0
        lax.fori_loop(0, 3, three_taps, 0)

    start_loads(0)

    barrier = pltpu.get_barrier_semaphore()

    def greet(cond, segment, chan):
        @pl.when(cond)
        def _():
            pl.semaphore_signal(barrier, inc=1, device_id=(segment, chan), device_id_type=MESH)
        return jnp.where(cond, 1, 0)

    greeted = greet(place > 0, seg, jnp.maximum(me - 2, 0))
    greeted += greet(place < length - 1, seg, jnp.minimum(me + 2, n - 1))
    greeted += greet(place >= 0, seg, partner)
    greeted += greet(seg > 0, jnp.maximum(seg - 1, 0), me)
    greeted += greet(seg < segments - 1, jnp.minimum(seg + 1, segments - 1), me)
    greeted += greet(seg >= 0, segments - 1 - seg, me)
    pl.semaphore_wait(barrier, greeted)

    def hop(k, j, h, way):
        target = (jnp.maximum(me - 2, 0), jnp.minimum(me + 2, n - 1), partner)[way]
        return pltpu.make_async_remote_copy(
            src_ref=g.at[k, j, h],
            dst_ref=g.at[k, j, h],
            send_sem=send_sem.at[way, j, h],
            recv_sem=recv_sem.at[k, j, h],
            device_id=(seg, target),
            device_id_type=MESH,
        )

    def give(t, kind, h):
        target = (jnp.minimum(seg + 1, segments - 1), segments - 1 - seg)[kind]
        return pltpu.make_async_remote_copy(
            src_ref=passed_out.at[t, h],
            dst_ref=g.at[2 * (t + 1) + kind, me, h],
            send_sem=pass_send.at[t, kind, h],
            recv_sem=pass_recv.at[t, kind, h],
            device_id=(target, me),
            device_id_type=MESH,
        )

    def multiply(k, conv, q, h, first):
        for i in range(2):
            part = g[k, 2 * q + i, h]
            high = part.astype(jnp.bfloat16)
            low = (part - high.astype(jnp.float32)).astype(jnp.bfloat16)
            operand[i * rows : (i + 1) * rows] = high
            operand[width + i * rows : width + (i + 1) * rows] = high
            operand[2 * width + i * rows : 2 * width + (i + 1) * rows] = low

        def group(m, _):
            product = jnp.dot(
                wv[conv, q, m], operand[...], preferred_element_type=jnp.float32
            )
            if first:
                acc[h, m] = product
            else:
                acc[h, m] += product
            return 0
        lax.fori_loop(0, 3, group, 0)

    def gather_and_multiply(k, conv, ready):
        for h in range(HALVES):
            ready(h)

            @pl.when(place < length - 1)
            def _():
                hop(k, me, h, 1).start()

            @pl.when(place > 0)
            def _():
                hop(k, me, h, 0).start()

            hop(k, me, h, 2).start()

        if k < 2:
            split_weights(conv)
            if conv == 0:
                start_loads(1)

        def own(h, _):
            hop(k, partner, h, 2).wait_recv()
            multiply(k, conv, place, h, True)
            return 0
        lax.fori_loop(0, HALVES, own, 0)

        def step(u, _):
            d = u // HALVES
            h = u % HALVES
            for side in range(2):
                q = place - d if side == 0 else place + d
                there = q >= 0 if side == 0 else q < length
                onward = place < length - 1 if side == 0 else place > 0
                mine = 2 * q + core

                @pl.when(there)
                def _():
                    hop(k, mine, h, 2).wait_recv()

                    @pl.when(onward)
                    def _():
                        hop(k, mine, h, 1 - side).start()
                    hop(k, mine, h, 2).start()

            def one(side, _):
                q = place - d + 2 * d * side

                @pl.when((q >= 0) & (q < length))
                def _():
                    hop(k, 2 * q + 1 - core, h, 2).wait_recv()
                    multiply(k, conv, q, h, False)
                return 0
            lax.fori_loop(0, 2, one, 0)
            return 0
        lax.fori_loop(HALVES, length * HALVES, step, 0)

        def drain(u, _):
            q = u // HALVES
            h = u % HALVES
            j = 2 * q + core
            hop(k, j, h, 2).wait_send()

            @pl.when((q <= place) & (place < length - 1))
            def _():
                hop(k, j, h, 1).wait_send()

            @pl.when((q >= place) & (place > 0))
            def _():
                hop(k, j, h, 0).wait_send()
            return 0
        lax.fori_loop(0, length * HALVES, drain, 0)

    def multiply_held(k, conv):
        for h in range(HALVES):
            multiply(k, conv, 0, h, True)

        def one(u, _):
            multiply(k, conv, u // HALVES, u % HALVES, False)
            return 0
        lax.fori_loop(HALVES, length * HALVES, one, 0)

    spot = lax.broadcasted_iota(jnp.int32, (blk, positions), 1)
    column = spot % COLS

    def placed(start):
        total = None
        for dx in (-1, 0, 1):
            column_sum = None
            for dy in (-1, 0, 1):
                at = pl.ds(pl.multiple_of((dx + 1) * rows + start, 8), blk)
                part = jnp.concatenate([acc[h, dy + 1, at, :] for h in range(HALVES)], axis=1)
                if dy:
                    part = pltpu.roll(part, (-dy * COLS) % positions, 1)
                    source = spot + dy * COLS
                    part = jnp.where((source >= 0) & (source < positions), part, 0.0)
                column_sum = part if column_sum is None else column_sum + part
            if dx:
                column_sum = pltpu.roll(column_sum, (-dx) % positions, 1)
                source = column + dx
                column_sum = jnp.where((source >= 0) & (source < COLS), column_sum, 0.0)
            total = column_sum if total is None else total + column_sum
        return total

    def over_rows(action):
        def one(i, _):
            start = pl.multiple_of(i * blk, 8)
            action(start, pl.ds(start, blk))
            return 0
        lax.fori_loop(0, rows // blk, one, 0)

    def halves_of(value):
        return [value[:, h * part_positions : (h + 1) * part_positions] for h in range(HALVES)]

    def nothing(h):
        pass

    for h in range(HALVES):
        cut = slice(h * part_positions, (h + 1) * part_positions)
        g[0, me, h] = resident[:, cut]

        @pl.when(jnp.logical_not(encoder))
        def _():
            g[1, me, h] = held_skip[:, cut]

    for t in range(ticks):
        k = 2 * t

        def input_ready(h):
            if t == 0:
                return

            @pl.when(seg > 0)
            def _():
                give(t - 1, 0, h).wait_recv()

            @pl.when(seg == 0)
            def _():
                g[k, me, h] = fresh[t - 1, :, h * part_positions : (h + 1) * part_positions]

        gather_and_multiply(k, 0, input_ready)

        def after_first(start, rows_of):
            value = placed(start)
            conv_first[rows_of, :] = value

            @pl.when(encoder)
            def _():
                for h, part in enumerate(halves_of(silu(value))):
                    g[k + 1, me, h, rows_of, :] = part
        over_rows(after_first)

        if t == 0:
            gather_and_multiply(1, 1, nothing)
        else:
            def operand_ready(h):
                @pl.when(jnp.logical_not(encoder))
                def _():
                    give(t - 1, 1, h).wait_recv()

            @pl.when(shares_input)
            def _():
                multiply_held(k, 1)

            @pl.when(jnp.logical_not(shares_input))
            def _():
                gather_and_multiply(k + 1, 1, operand_ready)

        def after_second(start, rows_of):
            value = placed(start)

            @pl.when(encoder)
            def _():
                for h, part in enumerate(halves_of(value)):
                    passed_out[t, h, rows_of, :] = g[k, me, h, rows_of, :] + part

            @pl.when(jnp.logical_not(encoder))
            def _():
                for h, part in enumerate(halves_of(silu(conv_first[rows_of, :] + value))):
                    passed_out[t, h, rows_of, :] = part
        over_rows(after_second)

        if t < ticks - 1:
            @pl.when(seg < segments - 1)
            def _():
                for h in range(HALVES):
                    give(t, 0, h).start()

            @pl.when(seg < half - 1)
            def _():
                for h in range(HALVES):
                    give(t, 1, h).start()

    for t in range(ticks - 1):
        for h in range(HALVES):
            @pl.when(seg < segments - 1)
            def _():
                give(t, 0, h).wait_send()

            @pl.when(seg < half - 1)
            def _():
                give(t, 1, h).wait_send()
    for h in range(HALVES):
        out_ref[:, h * part_positions : (h + 1) * part_positions] = passed_out[ticks - 1, h]


def body(segments, n, resident, held_skip, fresh, first_weight, second_weight):
    ticks = fresh.shape[0] + 1
    rows, positions = resident.shape[1:]
    part_positions = positions // HALVES
    length = n // 2
    width = 2 * rows
    vmem = pl.BlockSpec(memory_space=pltpu.VMEM)
    anywhere = pl.BlockSpec(memory_space=pl.ANY)
    out = pl.pallas_call(
        functools.partial(kernel, segments, n, ticks),
        out_shape=jax.ShapeDtypeStruct((rows, positions), jnp.float32),
        in_specs=[vmem, vmem, vmem, anywhere, anywhere],
        out_specs=vmem,
        scratch_shapes=[
            pltpu.VMEM((9, rows, length * width), jnp.float32),
            pltpu.VMEM((2, length, 3, 3 * rows, 3 * width), jnp.bfloat16),
            pltpu.VMEM((2 * ticks, n, HALVES, rows, part_positions), jnp.float32),
            pltpu.VMEM((3 * width, part_positions), jnp.bfloat16),
            pltpu.VMEM((HALVES, 3, 3 * rows, part_positions), jnp.float32),
            pltpu.VMEM((rows, positions), jnp.float32),
            pltpu.VMEM((ticks, HALVES, rows, part_positions), jnp.float32),
            pltpu.SemaphoreType.DMA((9,)),
            pltpu.SemaphoreType.DMA((2 * ticks, n, HALVES)),
            pltpu.SemaphoreType.DMA((3, n, HALVES)),
            pltpu.SemaphoreType.DMA((ticks - 1, 2, HALVES)),
            pltpu.SemaphoreType.DMA((ticks - 1, 2, HALVES)),
        ],
        compiler_params=pltpu.CompilerParams(
            collective_id=0, has_side_effects=True, vmem_limit_bytes=62 * 1024 * 1024
        ),
    )(resident[0], held_skip[0], fresh, first_weight, second_weight)
    return out[None]


def solution(mesh):
    return jax.shard_map(
        functools.partial(body, mesh.shape["segment"], mesh.shape["chan"]),
        mesh=mesh,
        in_specs=(
            P("segment", "chan", None),
            P("segment", "chan", None),
            P(None, "chan", None),
            P("segment", "chan", None),
            P("segment", "chan", None),
        ),
        out_specs=P("segment", "chan", None),
        check_vma=False,
    )
```

```python
import functools

import jax
import jax.numpy as jnp
from jax import lax
from jax.experimental import pallas as pl
from jax.experimental.pallas import tpu as pltpu
from jax.sharding import PartitionSpec as P

ROWS = 16
COLS = 32
MESH = pl.DeviceIdType.MESH


def silu(v):
    return v / (1.0 + jnp.exp(-v))


def block_of(rows):
    for size in (32, 40, 16):
        if rows % size == 0:
            return size
    return 8


HALVES = 2
QUARTERS = 4
UNITS = ((0, 1), (1, 1), (2, 2))


def kernel(
    segments, n, ticks,
    resident, held_skip, fresh, first_weight, second_weight, out_ref,
    stage, wv, g, operand, acc, conv_first, passed_out,
    w_sem, recv_sem, send_sem, direct_sem, pass_send, pass_recv,
):
    seg = lax.axis_index("segment")
    me = lax.axis_index("chan")
    place = me // 2
    core = me % 2
    partner = me + 1 - 2 * core
    length = n // 2
    half = segments // 2
    encoder = seg < half
    shares_input = seg == half
    rows, positions = resident.shape
    quarter = positions // QUARTERS
    width = 2 * rows
    channels = length * width
    blk = block_of(rows)
    split_blk = 32 if rows % 32 == 0 else rows

    def load(conv, tap):
        source = (first_weight, second_weight)[conv]
        columns = pl.ds(pl.multiple_of(tap * channels, 128), channels)
        return pltpu.make_async_copy(source.at[0, :, columns], stage.at[tap], w_sem.at[tap])

    def start_loads(conv):
        def one(tap, _):
            load(conv, tap).start()
            return 0
        lax.fori_loop(0, 9, one, 0)

    def split_weights(conv):
        def three_taps(y, _):
            for x in range(3):
                tap = 3 * y + x
                load(conv, tap).wait()

                def some_rows(i, _):
                    start = i * split_blk
                    if split_blk != rows:
                        start = pl.multiple_of(start, 16)
                    for q in range(length):
                        value = stage[tap, pl.ds(start, split_blk), q * width : (q + 1) * width]
                        high = value.astype(jnp.bfloat16)
                        low = (value - high.astype(jnp.float32)).astype(jnp.bfloat16)
                        spot = pl.ds(x * rows + start, split_blk)
                        if split_blk != rows:
                            spot = pl.ds(pl.multiple_of(x * rows + start, 16), split_blk)
                        wv[conv, q, y, spot, 0:width] = high
                        wv[conv, q, y, spot, width : 2 * width] = low
                        wv[conv, q, y, spot, 2 * width : 3 * width] = high
                    return 0
                if split_blk == rows:
                    some_rows(0, 0)
                else:
                    lax.fori_loop(0, rows // split_blk, some_rows, 0)
            return 0
        lax.fori_loop(0, 3, three_taps, 0)

    start_loads(0)

    barrier = pltpu.get_barrier_semaphore()

    def greet(cond, segment, chan):
        @pl.when(cond)
        def _():
            pl.semaphore_signal(barrier, inc=1, device_id=(segment, chan), device_id_type=MESH)
        return jnp.where(cond, 1, 0)

    def greet_line(q, _):
        greet(q != place, seg, 2 * q + core)
        return 0
    lax.fori_loop(0, length, greet_line, 0)
    greeted = length - 1
    greeted += greet(place >= 0, seg, partner)
    greeted += greet(seg > 0, jnp.maximum(seg - 1, 0), me)
    greeted += greet(seg < segments - 1, jnp.minimum(seg + 1, segments - 1), me)
    greeted += greet(seg >= 0, segments - 1 - seg, me)
    pl.semaphore_wait(barrier, greeted)

    def span(unit):
        return pl.ds(*UNITS[unit])

    def hop(k, j, unit, way):
        target = (jnp.maximum(me - 2, 0), jnp.minimum(me + 2, n - 1), partner)[way]
        return pltpu.make_async_remote_copy(
            src_ref=g.at[k, j, span(unit)],
            dst_ref=g.at[k, j, span(unit)],
            send_sem=send_sem.at[k % 2, way, j, unit],
            recv_sem=recv_sem.at[k, j, unit],
            device_id=(seg, target),
            device_id_type=MESH,
        )

    def direct(k, q):
        return pltpu.make_async_remote_copy(
            src_ref=g.at[k, me, span(0)],
            dst_ref=g.at[k, me, span(0)],
            send_sem=direct_sem.at[k % 2, q],
            recv_sem=recv_sem.at[k, me, 0],
            device_id=(seg, 2 * q + core),
            device_id_type=MESH,
        )

    def send_early(k):
        hop(k, me, 0, 2).start()

        def one(q, _):
            @pl.when(q != place)
            def _():
                direct(k, q).start()
            return 0
        lax.fori_loop(0, length, one, 0)

    def give(t, kind, unit):
        target = (jnp.minimum(seg + 1, segments - 1), segments - 1 - seg)[kind]
        return pltpu.make_async_remote_copy(
            src_ref=passed_out.at[t, span(unit)],
            dst_ref=g.at[2 * (t + 1) + kind, me, span(unit)],
            send_sem=pass_send.at[t, kind, unit],
            recv_sem=pass_recv.at[t, kind, unit],
            device_id=(target, me),
            device_id_type=MESH,
        )

    def give_unit(t, unit):
        @pl.when(seg < segments - 1)
        def _():
            give(t, 0, unit).start()

        @pl.when(seg < half - 1)
        def _():
            give(t, 1, unit).start()

    def clear():
        for h in range(HALVES):
            def one(m, _):
                acc[h, m] = jnp.zeros(acc.shape[2:], jnp.float32)
                return 0
            lax.fori_loop(0, 3, one, 0)

    def multiply(k, conv, q, h):
        for i in range(2):
            for c in range(2):
                part = g[k, 2 * q + i, 2 * h + c]
                high = part.astype(jnp.bfloat16)
                low = (part - high.astype(jnp.float32)).astype(jnp.bfloat16)
                cut = slice(c * quarter, (c + 1) * quarter)
                operand[i * rows : (i + 1) * rows, cut] = high
                operand[width + i * rows : width + (i + 1) * rows, cut] = high
                operand[2 * width + i * rows : 2 * width + (i + 1) * rows, cut] = low

        def group(m, _):
            acc[h, m] += jnp.dot(
                wv[conv, q, m], operand[...], preferred_element_type=jnp.float32
            )
            return 0
        lax.fori_loop(0, 3, group, 0)

    def gather_and_multiply(k, conv, ready, early):
        for unit in (1, 2):
            ready(unit)

            @pl.when(place < length - 1)
            def _():
                hop(k, me, unit, 1).start()

            @pl.when(place > 0)
            def _():
                hop(k, me, unit, 0).start()

            hop(k, me, unit, 2).start()

        if k < 2:
            split_weights(conv)
            if conv == 0:
                start_loads(1)
        clear()

        def step(d, h):
            unit = h + 1
            for side in range(2):
                q = place - d if side == 0 else place + d
                there = (d > 0) & (q >= 0 if side == 0 else q < length)
                onward = place < length - 1 if side == 0 else place > 0
                mine = 2 * q + core

                @pl.when(there)
                def _():
                    if h == 0:
                        hop(k, mine, 0, 2).wait_recv()
                        hop(k, mine, 0, 2).start()
                    hop(k, mine, unit, 2).wait_recv()

                    @pl.when(onward)
                    def _():
                        hop(k, mine, unit, 1 - side).start()
                    hop(k, mine, unit, 2).start()

            def one(side, _):
                q = place - d + 2 * d * side

                @pl.when((q >= 0) & (q < length) & ((d > 0) | (side == 0)))
                def _():
                    if h == 0:
                        hop(k, 2 * q + 1 - core, 0, 2).wait_recv()
                    hop(k, 2 * q + 1 - core, unit, 2).wait_recv()
                    multiply(k, conv, q, h)
                return 0
            lax.fori_loop(0, 2, one, 0)

        def both(d, _):
            step(d, 0)
            step(d, 1)
            return 0
        lax.fori_loop(0, length - 1, both, 0)
        step(jnp.int32(length - 1), 0)
        early()
        step(jnp.int32(length - 1), 1)

        def drain(q, _):
            j = 2 * q + core
            hop(k, j, 0, 2).wait_send()

            @pl.when(q != place)
            def _():
                direct(k, q).wait_send()

            for unit in (1, 2):
                hop(k, j, unit, 2).wait_send()

                @pl.when((q <= place) & (place < length - 1))
                def _():
                    hop(k, j, unit, 1).wait_send()

                @pl.when((q >= place) & (place > 0))
                def _():
                    hop(k, j, unit, 0).wait_send()
            return 0
        lax.fori_loop(0, length, drain, 0)

    def multiply_held(k, conv, early):
        clear()
        for h in range(HALVES):
            def one(q, _):
                multiply(k, conv, q, h)
                return 0
            lax.fori_loop(0, length, one, 0)
            if h == 0:
                early()

    def placed(start, halves):
        extent = 2 * quarter * halves
        spot = lax.broadcasted_iota(jnp.int32, (blk, extent), 1)
        column = spot % COLS
        total = None
        for dx in (-1, 0, 1):
            column_sum = None
            for dy in (-1, 0, 1):
                at = pl.ds(pl.multiple_of((dx + 1) * rows + start, 8), blk)
                part = jnp.concatenate([acc[h, dy + 1, at, :] for h in range(halves)], axis=1)
                if dy:
                    part = pltpu.roll(part, (-dy * COLS) % extent, 1)
                    source = spot + dy * COLS
                    part = jnp.where((source >= 0) & (source < extent), part, 0.0)
                column_sum = part if column_sum is None else column_sum + part
            if dx:
                column_sum = pltpu.roll(column_sum, (-dx) % extent, 1)
                source = column + dx
                column_sum = jnp.where((source >= 0) & (source < COLS), column_sum, 0.0)
            total = column_sum if total is None else total + column_sum
        return total

    def over_rows(action):
        def one(i, _):
            start = pl.multiple_of(i * blk, 8)
            action(start, pl.ds(start, blk))
            return 0
        lax.fori_loop(0, rows // blk, one, 0)

    def cut(c):
        return slice(c * quarter, (c + 1) * quarter)

    def finish_first(k, quarters, halves):
        def action(start, rows_of):
            value = placed(start, halves)
            for c in quarters:
                conv_first[c, rows_of, :] = value[:, cut(c)]

            @pl.when(encoder)
            def _():
                for c in quarters:
                    g[k + 1, me, c, rows_of, :] = silu(value[:, cut(c)])
        over_rows(action)

    def finish_second(t, quarters, halves):
        def action(start, rows_of):
            value = placed(start, halves)

            @pl.when(encoder)
            def _():
                for c in quarters:
                    passed_out[t, c, rows_of, :] = g[2 * t, me, c, rows_of, :] + value[:, cut(c)]

            @pl.when(jnp.logical_not(encoder))
            def _():
                for c in quarters:
                    passed_out[t, c, rows_of, :] = silu(conv_first[c, rows_of, :] + value[:, cut(c)])
        over_rows(action)

    for c in range(QUARTERS):
        g[0, me, c] = resident[:, cut(c)]

        @pl.when(jnp.logical_not(encoder))
        def _():
            g[1, me, c] = held_skip[:, cut(c)]

    send_early(0)
    for t in range(ticks):
        k = 2 * t

        def input_ready(unit):
            if t:
                @pl.when(seg > 0)
                def _():
                    give(t - 1, 0, unit).wait_recv()

        def operand_ready(unit):
            if t:
                @pl.when(jnp.logical_not(encoder))
                def _():
                    give(t - 1, 1, unit).wait_recv()

        def early_first():
            finish_first(k, (0,), 1)
            if t == 0:
                send_early(1)
            else:
                @pl.when(jnp.logical_not(shares_input))
                def _():
                    operand_ready(0)
                    send_early(k + 1)

        def early_second():
            finish_second(t, (0,), 1)
            if t < ticks - 1:
                give_unit(t, 0)

                @pl.when(seg == 0)
                def _():
                    for c in range(QUARTERS):
                        g[k + 2, me, c] = fresh[t, :, cut(c)]
                    send_early(k + 2)

        if t:
            @pl.when(seg > 0)
            def _():
                give(t - 1, 0, 0).wait_recv()
                send_early(k)

        gather_and_multiply(k, 0, input_ready, early_first)
        finish_first(k, (1, 2, 3), 2)

        if t == 0:
            gather_and_multiply(1, 1, operand_ready, early_second)
        else:
            @pl.when(shares_input)
            def _():
                multiply_held(k, 1, early_second)

            @pl.when(jnp.logical_not(shares_input))
            def _():
                gather_and_multiply(k + 1, 1, operand_ready, early_second)
        finish_second(t, (1, 2, 3), 2)
        if t < ticks - 1:
            give_unit(t, 1)
            give_unit(t, 2)

    for t in range(ticks - 1):
        for unit in range(len(UNITS)):
            @pl.when(seg < segments - 1)
            def _():
                give(t, 0, unit).wait_send()

            @pl.when(seg < half - 1)
            def _():
                give(t, 1, unit).wait_send()
    for c in range(QUARTERS):
        out_ref[:, cut(c)] = passed_out[ticks - 1, c]


def body(segments, n, resident, held_skip, fresh, first_weight, second_weight):
    ticks = fresh.shape[0] + 1
    rows, positions = resident.shape[1:]
    quarter = positions // QUARTERS
    length = n // 2
    width = 2 * rows
    vmem = pl.BlockSpec(memory_space=pltpu.VMEM)
    anywhere = pl.BlockSpec(memory_space=pl.ANY)
    out = pl.pallas_call(
        functools.partial(kernel, segments, n, ticks),
        out_shape=jax.ShapeDtypeStruct((rows, positions), jnp.float32),
        in_specs=[vmem, vmem, vmem, anywhere, anywhere],
        out_specs=vmem,
        scratch_shapes=[
            pltpu.VMEM((9, rows, length * width), jnp.float32),
            pltpu.VMEM((2, length, 3, 3 * rows, 3 * width), jnp.bfloat16),
            pltpu.VMEM((2 * ticks, n, QUARTERS, rows, quarter), jnp.float32),
            pltpu.VMEM((3 * width, 2 * quarter), jnp.bfloat16),
            pltpu.VMEM((HALVES, 3, 3 * rows, 2 * quarter), jnp.float32),
            pltpu.VMEM((QUARTERS, rows, quarter), jnp.float32),
            pltpu.VMEM((ticks, QUARTERS, rows, quarter), jnp.float32),
            pltpu.SemaphoreType.DMA((9,)),
            pltpu.SemaphoreType.DMA((2 * ticks, n, len(UNITS))),
            pltpu.SemaphoreType.DMA((2, 3, n, len(UNITS))),
            pltpu.SemaphoreType.DMA((2, length)),
            pltpu.SemaphoreType.DMA((ticks - 1, 2, len(UNITS))),
            pltpu.SemaphoreType.DMA((ticks - 1, 2, len(UNITS))),
        ],
        compiler_params=pltpu.CompilerParams(
            collective_id=0, has_side_effects=True, vmem_limit_bytes=62 * 1024 * 1024
        ),
    )(resident[0], held_skip[0], fresh, first_weight, second_weight)
    return out[None]


def solution(mesh):
    return jax.shard_map(
        functools.partial(body, mesh.shape["segment"], mesh.shape["chan"]),
        mesh=mesh,
        in_specs=(
            P("segment", "chan", None),
            P("segment", "chan", None),
            P(None, "chan", None),
            P("segment", "chan", None),
            P("segment", "chan", None),
        ),
        out_specs=P("segment", "chan", None),
        check_vma=False,
    )
```

```python
import functools

import jax
import jax.numpy as jnp
from jax import lax
from jax.experimental import pallas as pl
from jax.experimental.pallas import tpu as pltpu
from jax.sharding import PartitionSpec as P

ROWS = 16
COLS = 32
MESH = pl.DeviceIdType.MESH


def silu(v):
    return v / (1.0 + jnp.exp(-v))


def block_of(rows):
    for size in (32, 40, 16):
        if rows % size == 0:
            return size
    return 8


HALVES = 2


def kernel(
    segments, n, ticks,
    resident, held_skip, fresh, first_weight, second_weight, out_ref,
    stage, wv, g, operand, acc, conv_first, passed_out,
    w_sem, recv_sem, send_sem, pass_send, pass_recv,
):
    seg = lax.axis_index("segment")
    me = lax.axis_index("chan")
    place = me // 2
    core = me % 2
    partner = me + 1 - 2 * core
    length = n // 2
    half = segments // 2
    encoder = seg < half
    shares_input = seg == half
    rows, positions = resident.shape
    part_positions = positions // HALVES
    width = 2 * rows
    channels = length * width
    blk = block_of(rows)
    split_blk = 32 if rows % 32 == 0 else rows

    def load(conv, tap):
        source = (first_weight, second_weight)[conv]
        columns = pl.ds(pl.multiple_of(tap * channels, 128), channels)
        return pltpu.make_async_copy(source.at[0, :, columns], stage.at[tap], w_sem.at[tap])

    def start_loads(conv):
        def one(tap, _):
            load(conv, tap).start()
            return 0
        lax.fori_loop(0, 9, one, 0)

    def split_weights(conv):
        def three_taps(y, _):
            for x in range(3):
                tap = 3 * y + x
                load(conv, tap).wait()

                def some_rows(i, _):
                    start = i * split_blk
                    if split_blk != rows:
                        start = pl.multiple_of(start, 16)
                    for q in range(length):
                        value = stage[tap, pl.ds(start, split_blk), q * width : (q + 1) * width]
                        high = value.astype(jnp.bfloat16)
                        low = (value - high.astype(jnp.float32)).astype(jnp.bfloat16)
                        spot = pl.ds(x * rows + start, split_blk)
                        if split_blk != rows:
                            spot = pl.ds(pl.multiple_of(x * rows + start, 16), split_blk)
                        wv[conv, q, y, spot, 0:width] = high
                        wv[conv, q, y, spot, width : 2 * width] = low
                        wv[conv, q, y, spot, 2 * width : 3 * width] = high
                    return 0
                if split_blk == rows:
                    some_rows(0, 0)
                else:
                    lax.fori_loop(0, rows // split_blk, some_rows, 0)
            return 0
        lax.fori_loop(0, 3, three_taps, 0)

    start_loads(0)

    barrier = pltpu.get_barrier_semaphore()

    def greet(cond, segment, chan):
        @pl.when(cond)
        def _():
            pl.semaphore_signal(barrier, inc=1, device_id=(segment, chan), device_id_type=MESH)
        return jnp.where(cond, 1, 0)

    greeted = greet(place > 0, seg, jnp.maximum(me - 2, 0))
    greeted += greet(place < length - 1, seg, jnp.minimum(me + 2, n - 1))
    greeted += greet(place >= 0, seg, partner)
    greeted += greet(seg > 0, jnp.maximum(seg - 1, 0), me)
    greeted += greet(seg < segments - 1, jnp.minimum(seg + 1, segments - 1), me)
    greeted += greet(seg >= 0, segments - 1 - seg, me)
    pl.semaphore_wait(barrier, greeted)

    def hop(k, j, h, way):
        target = (jnp.maximum(me - 2, 0), jnp.minimum(me + 2, n - 1), partner)[way]
        return pltpu.make_async_remote_copy(
            src_ref=g.at[k, j, h],
            dst_ref=g.at[k, j, h],
            send_sem=send_sem.at[k % 2, way, j, h],
            recv_sem=recv_sem.at[k, j, h],
            device_id=(seg, target),
            device_id_type=MESH,
        )

    def give(t, kind, h):
        target = (jnp.minimum(seg + 1, segments - 1), segments - 1 - seg)[kind]
        return pltpu.make_async_remote_copy(
            src_ref=passed_out.at[t, h],
            dst_ref=g.at[2 * (t + 1) + kind, me, h],
            send_sem=pass_send.at[t, kind, h],
            recv_sem=pass_recv.at[t, kind, h],
            device_id=(target, me),
            device_id_type=MESH,
        )

    def multiply(k, conv, q, h, first):
        for i in range(2):
            part = g[k, 2 * q + i, h]
            high = part.astype(jnp.bfloat16)
            low = (part - high.astype(jnp.float32)).astype(jnp.bfloat16)
            operand[i * rows : (i + 1) * rows] = high
            operand[width + i * rows : width + (i + 1) * rows] = high
            operand[2 * width + i * rows : 2 * width + (i + 1) * rows] = low

        def group(m, _):
            product = jnp.dot(
                wv[conv, q, m], operand[...], preferred_element_type=jnp.float32
            )
            if first:
                acc[h, m] = product
            else:
                acc[h, m] += product
            return 0
        lax.fori_loop(0, 3, group, 0)

    def drain(k):
        def one(u, _):
            q = u // HALVES
            h = u % HALVES
            j = 2 * q + core
            hop(k, j, h, 2).wait_send()

            @pl.when((q <= place) & (place < length - 1))
            def _():
                hop(k, j, h, 1).wait_send()

            @pl.when((q >= place) & (place > 0))
            def _():
                hop(k, j, h, 0).wait_send()
            return 0
        lax.fori_loop(0, length * HALVES, one, 0)

    def gather_and_multiply(k, conv, ready):
        if k >= 2:
            drain(k - 2)
        for h in range(HALVES):
            ready(h)

            @pl.when(place < length - 1)
            def _():
                hop(k, me, h, 1).start()

            @pl.when(place > 0)
            def _():
                hop(k, me, h, 0).start()

            hop(k, me, h, 2).start()

        if k < 2:
            split_weights(conv)
            if conv == 0:
                start_loads(1)

        def own(h, _):
            hop(k, partner, h, 2).wait_recv()
            multiply(k, conv, place, h, True)
            return 0
        lax.fori_loop(0, HALVES, own, 0)

        def step(u, _):
            d = u // HALVES
            h = u % HALVES
            for side in range(2):
                q = place - d if side == 0 else place + d
                there = q >= 0 if side == 0 else q < length
                onward = place < length - 1 if side == 0 else place > 0
                mine = 2 * q + core

                @pl.when(there)
                def _():
                    hop(k, mine, h, 2).wait_recv()

                    @pl.when(onward)
                    def _():
                        hop(k, mine, h, 1 - side).start()
                    hop(k, mine, h, 2).start()

            def one(side, _):
                q = place - d + 2 * d * side

                @pl.when((q >= 0) & (q < length))
                def _():
                    hop(k, 2 * q + 1 - core, h, 2).wait_recv()
                    multiply(k, conv, q, h, False)
                return 0
            lax.fori_loop(0, 2, one, 0)
            return 0
        lax.fori_loop(HALVES, length * HALVES, step, 0)

    def multiply_held(k, conv):
        for h in range(HALVES):
            multiply(k, conv, 0, h, True)

        def one(u, _):
            multiply(k, conv, u // HALVES, u % HALVES, False)
            return 0
        lax.fori_loop(HALVES, length * HALVES, one, 0)

    spot = lax.broadcasted_iota(jnp.int32, (blk, positions), 1)
    column = spot % COLS

    def placed(start):
        total = None
        for dx in (-1, 0, 1):
            column_sum = None
            for dy in (-1, 0, 1):
                at = pl.ds(pl.multiple_of((dx + 1) * rows + start, 8), blk)
                part = jnp.concatenate([acc[h, dy + 1, at, :] for h in range(HALVES)], axis=1)
                if dy:
                    part = pltpu.roll(part, (-dy * COLS) % positions, 1)
                    source = spot + dy * COLS
                    part = jnp.where((source >= 0) & (source < positions), part, 0.0)
                column_sum = part if column_sum is None else column_sum + part
            if dx:
                column_sum = pltpu.roll(column_sum, (-dx) % positions, 1)
                source = column + dx
                column_sum = jnp.where((source >= 0) & (source < COLS), column_sum, 0.0)
            total = column_sum if total is None else total + column_sum
        return total

    def over_rows(action):
        def one(i, _):
            start = pl.multiple_of(i * blk, 8)
            action(start, pl.ds(start, blk))
            return 0
        lax.fori_loop(0, rows // blk, one, 0)

    def halves_of(value):
        return [value[:, h * part_positions : (h + 1) * part_positions] for h in range(HALVES)]

    def nothing(h):
        pass

    for h in range(HALVES):
        cut = slice(h * part_positions, (h + 1) * part_positions)
        g[0, me, h] = resident[:, cut]

        @pl.when(jnp.logical_not(encoder))
        def _():
            g[1, me, h] = held_skip[:, cut]

    for t in range(ticks):
        k = 2 * t

        def input_ready(h):
            if t == 0:
                return

            @pl.when(seg > 0)
            def _():
                give(t - 1, 0, h).wait_recv()

            @pl.when(seg == 0)
            def _():
                g[k, me, h] = fresh[t - 1, :, h * part_positions : (h + 1) * part_positions]

        gather_and_multiply(k, 0, input_ready)

        def after_first(start, rows_of):
            value = placed(start)
            conv_first[rows_of, :] = value

            @pl.when(encoder)
            def _():
                for h, part in enumerate(halves_of(silu(value))):
                    g[k + 1, me, h, rows_of, :] = part
        over_rows(after_first)

        if t == 0:
            gather_and_multiply(1, 1, nothing)
        else:
            def operand_ready(h):
                @pl.when(jnp.logical_not(encoder))
                def _():
                    give(t - 1, 1, h).wait_recv()

            @pl.when(shares_input)
            def _():
                if t == 1:
                    drain(1)
                multiply_held(k, 1)

            @pl.when(jnp.logical_not(shares_input))
            def _():
                gather_and_multiply(k + 1, 1, operand_ready)

        def after_second(start, rows_of):
            value = placed(start)

            @pl.when(encoder)
            def _():
                for h, part in enumerate(halves_of(value)):
                    passed_out[t, h, rows_of, :] = g[k, me, h, rows_of, :] + part

            @pl.when(jnp.logical_not(encoder))
            def _():
                for h, part in enumerate(halves_of(silu(conv_first[rows_of, :] + value))):
                    passed_out[t, h, rows_of, :] = part
        over_rows(after_second)

        if t < ticks - 1:
            @pl.when(seg < segments - 1)
            def _():
                for h in range(HALVES):
                    give(t, 0, h).start()

            @pl.when(seg < half - 1)
            def _():
                for h in range(HALVES):
                    give(t, 1, h).start()

    drain(2 * ticks - 2)

    @pl.when(jnp.logical_not(shares_input) | (ticks == 1))
    def _():
        drain(2 * ticks - 1)

    for t in range(ticks - 1):
        for h in range(HALVES):
            @pl.when(seg < segments - 1)
            def _():
                give(t, 0, h).wait_send()

            @pl.when(seg < half - 1)
            def _():
                give(t, 1, h).wait_send()
    for h in range(HALVES):
        out_ref[:, h * part_positions : (h + 1) * part_positions] = passed_out[ticks - 1, h]


def body(segments, n, resident, held_skip, fresh, first_weight, second_weight):
    ticks = fresh.shape[0] + 1
    rows, positions = resident.shape[1:]
    part_positions = positions // HALVES
    length = n // 2
    width = 2 * rows
    vmem = pl.BlockSpec(memory_space=pltpu.VMEM)
    anywhere = pl.BlockSpec(memory_space=pl.ANY)
    out = pl.pallas_call(
        functools.partial(kernel, segments, n, ticks),
        out_shape=jax.ShapeDtypeStruct((rows, positions), jnp.float32),
        in_specs=[vmem, vmem, vmem, anywhere, anywhere],
        out_specs=vmem,
        scratch_shapes=[
            pltpu.VMEM((9, rows, length * width), jnp.float32),
            pltpu.VMEM((2, length, 3, 3 * rows, 3 * width), jnp.bfloat16),
            pltpu.VMEM((2 * ticks, n, HALVES, rows, part_positions), jnp.float32),
            pltpu.VMEM((3 * width, part_positions), jnp.bfloat16),
            pltpu.VMEM((HALVES, 3, 3 * rows, part_positions), jnp.float32),
            pltpu.VMEM((rows, positions), jnp.float32),
            pltpu.VMEM((ticks, HALVES, rows, part_positions), jnp.float32),
            pltpu.SemaphoreType.DMA((9,)),
            pltpu.SemaphoreType.DMA((2 * ticks, n, HALVES)),
            pltpu.SemaphoreType.DMA((2, 3, n, HALVES)),
            pltpu.SemaphoreType.DMA((ticks - 1, 2, HALVES)),
            pltpu.SemaphoreType.DMA((ticks - 1, 2, HALVES)),
        ],
        compiler_params=pltpu.CompilerParams(
            collective_id=0, has_side_effects=True, vmem_limit_bytes=62 * 1024 * 1024
        ),
    )(resident[0], held_skip[0], fresh, first_weight, second_weight)
    return out[None]


def solution(mesh):
    return jax.shard_map(
        functools.partial(body, mesh.shape["segment"], mesh.shape["chan"]),
        mesh=mesh,
        in_specs=(
            P("segment", "chan", None),
            P("segment", "chan", None),
            P(None, "chan", None),
            P("segment", "chan", None),
            P("segment", "chan", None),
        ),
        out_specs=P("segment", "chan", None),
        check_vma=False,
    )
```

```python
import functools

import jax
import jax.numpy as jnp
from jax import lax
from jax.experimental import pallas as pl
from jax.experimental.pallas import tpu as pltpu
from jax.sharding import PartitionSpec as P

ROWS = 16
COLS = 32
MESH = pl.DeviceIdType.MESH


def silu(v):
    return v / (1.0 + jnp.exp(-v))


def block_of(rows):
    for size in (32, 40, 16):
        if rows % size == 0:
            return size
    return 8


HALVES = 2


def kernel(
    segments, n, ticks,
    resident, held_skip, fresh, first_weight, second_weight, out_ref,
    stage, wv, g, operand, acc, conv_first, passed_out,
    w_sem, recv_sem, send_sem, pass_send, pass_recv,
):
    seg = lax.axis_index("segment")
    me = lax.axis_index("chan")
    place = me // 2
    core = me % 2
    partner = me + 1 - 2 * core
    length = n // 2
    half = segments // 2
    encoder = seg < half
    shares_input = seg == half
    rows, positions = resident.shape
    part_positions = positions // HALVES
    width = 2 * rows
    channels = length * width
    blk = block_of(rows)
    split_blk = 32 if rows % 32 == 0 else rows

    def load(conv, tap):
        source = (first_weight, second_weight)[conv]
        columns = pl.ds(pl.multiple_of(tap * channels, 128), channels)
        return pltpu.make_async_copy(source.at[0, :, columns], stage.at[tap], w_sem.at[tap])

    def start_loads(conv):
        def one(tap, _):
            load(conv, tap).start()
            return 0
        lax.fori_loop(0, 9, one, 0)

    def split_weights(conv):
        def three_taps(y, _):
            for x in range(3):
                tap = 3 * y + x
                load(conv, tap).wait()

                def some_rows(i, _):
                    start = i * split_blk
                    if split_blk != rows:
                        start = pl.multiple_of(start, 16)
                    for q in range(length):
                        value = stage[tap, pl.ds(start, split_blk), q * width : (q + 1) * width]
                        high = value.astype(jnp.bfloat16)
                        low = (value - high.astype(jnp.float32)).astype(jnp.bfloat16)
                        spot = pl.ds(x * rows + start, split_blk)
                        if split_blk != rows:
                            spot = pl.ds(pl.multiple_of(x * rows + start, 16), split_blk)
                        wv[conv, q, y, spot, 0:width] = high
                        wv[conv, q, y, spot, width : 2 * width] = low
                        wv[conv, q, y, spot, 2 * width : 3 * width] = high
                    return 0
                if split_blk == rows:
                    some_rows(0, 0)
                else:
                    lax.fori_loop(0, rows // split_blk, some_rows, 0)
            return 0
        lax.fori_loop(0, 3, three_taps, 0)

    start_loads(0)

    barrier = pltpu.get_barrier_semaphore()

    def greet(cond, segment, chan):
        @pl.when(cond)
        def _():
            pl.semaphore_signal(barrier, inc=1, device_id=(segment, chan), device_id_type=MESH)
        return jnp.where(cond, 1, 0)

    greeted = greet(place > 0, seg, jnp.maximum(me - 2, 0))
    greeted += greet(place < length - 1, seg, jnp.minimum(me + 2, n - 1))
    greeted += greet(place >= 0, seg, partner)
    greeted += greet(seg > 0, jnp.maximum(seg - 1, 0), me)
    greeted += greet(seg < segments - 1, jnp.minimum(seg + 1, segments - 1), me)
    greeted += greet(seg >= 0, segments - 1 - seg, me)
    pl.semaphore_wait(barrier, greeted)

    def hop(k, j, h, way):
        target = (jnp.maximum(me - 2, 0), jnp.minimum(me + 2, n - 1), partner)[way]
        return pltpu.make_async_remote_copy(
            src_ref=g.at[k, j, h],
            dst_ref=g.at[k, j, h],
            send_sem=send_sem.at[k % 2, way, j, h],
            recv_sem=recv_sem.at[k, j, h],
            device_id=(seg, target),
            device_id_type=MESH,
        )

    def give(t, kind, h):
        target = (jnp.minimum(seg + 1, segments - 1), segments - 1 - seg)[kind]
        return pltpu.make_async_remote_copy(
            src_ref=passed_out.at[t, h],
            dst_ref=g.at[2 * (t + 1) + kind, me, h],
            send_sem=pass_send.at[t, kind, h],
            recv_sem=pass_recv.at[t, kind, h],
            device_id=(target, me),
            device_id_type=MESH,
        )

    def multiply(k, conv, q, h, first):
        for i in range(2):
            part = g[k, 2 * q + i, h]
            high = part.astype(jnp.bfloat16)
            low = (part - high.astype(jnp.float32)).astype(jnp.bfloat16)
            operand[i * rows : (i + 1) * rows] = high
            operand[width + i * rows : width + (i + 1) * rows] = high
            operand[2 * width + i * rows : 2 * width + (i + 1) * rows] = low

        def group(m, _):
            product = jnp.dot(
                wv[conv, q, m], operand[...], preferred_element_type=jnp.float32
            )
            if first:
                acc[h, m] = product
            else:
                acc[h, m] += product
            return 0
        lax.fori_loop(0, 3, group, 0)

    def drain(k):
        def one(u, _):
            q = u // HALVES
            h = u % HALVES
            j = 2 * q + core
            hop(k, j, h, 2).wait_send()

            @pl.when((q <= place) & (place < length - 1))
            def _():
                hop(k, j, h, 1).wait_send()

            @pl.when((q >= place) & (place > 0))
            def _():
                hop(k, j, h, 0).wait_send()
            return 0
        lax.fori_loop(0, length * HALVES, one, 0)

    def gather_and_multiply(k, conv, ready):
        if k >= 2:
            drain(k - 2)
        for h in range(HALVES):
            ready(h)

            @pl.when(place < length - 1)
            def _():
                hop(k, me, h, 1).start()

            @pl.when(place > 0)
            def _():
                hop(k, me, h, 0).start()

            hop(k, me, h, 2).start()

        if k < 2:
            split_weights(conv)
            if conv == 0:
                start_loads(1)

        def own(h, _):
            hop(k, partner, h, 2).wait_recv()
            multiply(k, conv, place, h, True)
            return 0
        lax.fori_loop(0, HALVES, own, 0)

        inner = jnp.where(place < length // 2, 1, -1)

        def step(u, _):
            d = u // (2 * HALVES) + 1
            turn = (u // HALVES) % 2
            h = u % HALVES
            way = jnp.where(turn == 0, inner, -inner)
            q = place + way * d
            mine = 2 * q + core

            @pl.when((q >= 0) & (q < length))
            def _():
                hop(k, mine, h, 2).wait_recv()

                @pl.when((way > 0) & (place > 0))
                def _():
                    hop(k, mine, h, 0).start()

                @pl.when((way < 0) & (place < length - 1))
                def _():
                    hop(k, mine, h, 1).start()
                hop(k, mine, h, 2).start()
                hop(k, 2 * q + 1 - core, h, 2).wait_recv()
                multiply(k, conv, q, h, False)
            return 0
        lax.fori_loop(0, (length - 1) * 2 * HALVES, step, 0)

    def multiply_held(k, conv):
        for h in range(HALVES):
            multiply(k, conv, 0, h, True)

        def one(u, _):
            multiply(k, conv, u // HALVES, u % HALVES, False)
            return 0
        lax.fori_loop(HALVES, length * HALVES, one, 0)

    spot = lax.broadcasted_iota(jnp.int32, (blk, positions), 1)
    column = spot % COLS

    def placed(start):
        total = None
        for dx in (-1, 0, 1):
            column_sum = None
            for dy in (-1, 0, 1):
                at = pl.ds(pl.multiple_of((dx + 1) * rows + start, 8), blk)
                part = jnp.concatenate([acc[h, dy + 1, at, :] for h in range(HALVES)], axis=1)
                if dy:
                    part = pltpu.roll(part, (-dy * COLS) % positions, 1)
                    source = spot + dy * COLS
                    part = jnp.where((source >= 0) & (source < positions), part, 0.0)
                column_sum = part if column_sum is None else column_sum + part
            if dx:
                column_sum = pltpu.roll(column_sum, (-dx) % positions, 1)
                source = column + dx
                column_sum = jnp.where((source >= 0) & (source < COLS), column_sum, 0.0)
            total = column_sum if total is None else total + column_sum
        return total

    def over_rows(action):
        def one(i, _):
            start = pl.multiple_of(i * blk, 8)
            action(start, pl.ds(start, blk))
            return 0
        lax.fori_loop(0, rows // blk, one, 0)

    def halves_of(value):
        return [value[:, h * part_positions : (h + 1) * part_positions] for h in range(HALVES)]

    def nothing(h):
        pass

    for h in range(HALVES):
        cut = slice(h * part_positions, (h + 1) * part_positions)
        g[0, me, h] = resident[:, cut]

        @pl.when(jnp.logical_not(encoder))
        def _():
            g[1, me, h] = held_skip[:, cut]

    for t in range(ticks):
        k = 2 * t

        def input_ready(h):
            if t == 0:
                return

            @pl.when(seg > 0)
            def _():
                give(t - 1, 0, h).wait_recv()

            @pl.when(seg == 0)
            def _():
                g[k, me, h] = fresh[t - 1, :, h * part_positions : (h + 1) * part_positions]

        gather_and_multiply(k, 0, input_ready)

        def after_first(start, rows_of):
            value = placed(start)
            conv_first[rows_of, :] = value

            @pl.when(encoder)
            def _():
                for h, part in enumerate(halves_of(silu(value))):
                    g[k + 1, me, h, rows_of, :] = part
        over_rows(after_first)

        if t == 0:
            gather_and_multiply(1, 1, nothing)
        else:
            def operand_ready(h):
                @pl.when(jnp.logical_not(encoder))
                def _():
                    give(t - 1, 1, h).wait_recv()

            @pl.when(shares_input)
            def _():
                if t == 1:
                    drain(1)
                multiply_held(k, 1)

            @pl.when(jnp.logical_not(shares_input))
            def _():
                gather_and_multiply(k + 1, 1, operand_ready)

        def after_second(start, rows_of):
            value = placed(start)

            @pl.when(encoder)
            def _():
                for h, part in enumerate(halves_of(value)):
                    passed_out[t, h, rows_of, :] = g[k, me, h, rows_of, :] + part

            @pl.when(jnp.logical_not(encoder))
            def _():
                for h, part in enumerate(halves_of(silu(conv_first[rows_of, :] + value))):
                    passed_out[t, h, rows_of, :] = part
        over_rows(after_second)

        if t < ticks - 1:
            @pl.when(seg < segments - 1)
            def _():
                for h in range(HALVES):
                    give(t, 0, h).start()

            @pl.when(seg < half - 1)
            def _():
                for h in range(HALVES):
                    give(t, 1, h).start()

    drain(2 * ticks - 2)

    @pl.when(jnp.logical_not(shares_input) | (ticks == 1))
    def _():
        drain(2 * ticks - 1)

    for t in range(ticks - 1):
        for h in range(HALVES):
            @pl.when(seg < segments - 1)
            def _():
                give(t, 0, h).wait_send()

            @pl.when(seg < half - 1)
            def _():
                give(t, 1, h).wait_send()
    for h in range(HALVES):
        out_ref[:, h * part_positions : (h + 1) * part_positions] = passed_out[ticks - 1, h]


def body(segments, n, resident, held_skip, fresh, first_weight, second_weight):
    ticks = fresh.shape[0] + 1
    rows, positions = resident.shape[1:]
    part_positions = positions // HALVES
    length = n // 2
    width = 2 * rows
    vmem = pl.BlockSpec(memory_space=pltpu.VMEM)
    anywhere = pl.BlockSpec(memory_space=pl.ANY)
    out = pl.pallas_call(
        functools.partial(kernel, segments, n, ticks),
        out_shape=jax.ShapeDtypeStruct((rows, positions), jnp.float32),
        in_specs=[vmem, vmem, vmem, anywhere, anywhere],
        out_specs=vmem,
        scratch_shapes=[
            pltpu.VMEM((9, rows, length * width), jnp.float32),
            pltpu.VMEM((2, length, 3, 3 * rows, 3 * width), jnp.bfloat16),
            pltpu.VMEM((2 * ticks, n, HALVES, rows, part_positions), jnp.float32),
            pltpu.VMEM((3 * width, part_positions), jnp.bfloat16),
            pltpu.VMEM((HALVES, 3, 3 * rows, part_positions), jnp.float32),
            pltpu.VMEM((rows, positions), jnp.float32),
            pltpu.VMEM((ticks, HALVES, rows, part_positions), jnp.float32),
            pltpu.SemaphoreType.DMA((9,)),
            pltpu.SemaphoreType.DMA((2 * ticks, n, HALVES)),
            pltpu.SemaphoreType.DMA((2, 3, n, HALVES)),
            pltpu.SemaphoreType.DMA((ticks - 1, 2, HALVES)),
            pltpu.SemaphoreType.DMA((ticks - 1, 2, HALVES)),
        ],
        compiler_params=pltpu.CompilerParams(
            collective_id=0, has_side_effects=True, vmem_limit_bytes=62 * 1024 * 1024
        ),
    )(resident[0], held_skip[0], fresh, first_weight, second_weight)
    return out[None]


def solution(mesh):
    return jax.shard_map(
        functools.partial(body, mesh.shape["segment"], mesh.shape["chan"]),
        mesh=mesh,
        in_specs=(
            P("segment", "chan", None),
            P("segment", "chan", None),
            P(None, "chan", None),
            P("segment", "chan", None),
            P("segment", "chan", None),
        ),
        out_specs=P("segment", "chan", None),
        check_vma=False,
    )
```
